32 devices in a mesh: dp: 8 (over z, y), tensor: 4 (over x, core).
Axes of the slice: x: 2, y: 2, z: 4, core: 2. Of those that a mesh axis runs over, the one named last changes fastest.
Arguments:
- tokens: bfloat16 [16384, 1024], P(('dp', 'tensor')), may hold values from -6 to 6
- cotangent: bfloat16 [16384, 1024], P(('dp', 'tensor')), may hold values from -6 to 6
- segment_ids: int32 [16384], P('dp'), may hold values from 0 to 1023, as said below
- positions: int32 [16384], P('dp'), may hold values from 0 to 1023, as said below
- attention_entry: float32 [1024, 3, 1024], P('dp', None, 'tensor'), may hold values from -0.1875 to 0.1875
- attention_exit: float32 [1024, 1024], P('tensor', 'dp'), may hold values from -0.375 to 0.375
- feedforward_entry: float32 [1024, 2, 2624], P('dp', None, 'tensor'), may hold values from -0.1875 to 0.1875
- feedforward_exit: float32 [2624, 1024], P('tensor', 'dp'), may hold values from -0.125 to 0.125
- norm_gains: float32 [2, 1024], P(None, 'dp'), may hold values from 0.5 to 1.5
- momentum_attention_entry: float32 [1024, 3, 1024], P('dp', None, 'tensor'), may hold values from -40 to 40
- momentum_attention_exit: float32 [1024, 1024], P('tensor', 'dp'), may hold values from -40 to 40
- momentum_feedforward_entry: float32 [1024, 2, 2624], P('dp', None, 'tensor'), may hold values from -40 to 40
- momentum_feedforward_exit: float32 [2624, 1024], P('tensor', 'dp'), may hold values from -40 to 40
- momentum_norm_gains: float32 [2, 1024], P(None, 'dp'), may hold values from -40 to 40
- variance_attention_entry: float32 [1024, 3, 1024], P('dp', None, 'tensor'), may hold values from 32.768 to 819.2
- variance_attention_exit: float32 [1024, 1024], P('tensor', 'dp'), may hold values from 32.768 to 819.2
- variance_feedforward_entry: float32 [1024, 2, 2624], P('dp', None, 'tensor'), may hold values from 32.768 to 819.2
- variance_feedforward_exit: float32 [2624, 1024], P('tensor', 'dp'), may hold values from 32.768 to 819.2
- variance_norm_gains: float32 [2, 1024], P(None, 'dp'), may hold values from 32.768 to 819.2
Outputs:
- block_output: bfloat16 [16384, 1024], P(('dp', 'tensor'))
- input_gradient: float32 [16384, 1024], P(('dp', 'tensor'))
- attention_entry_gradient: float32 [1024, 3, 1024], P('dp', None, 'tensor')
- attention_entry_updated: float32 [1024, 3, 1024], P('dp', None, 'tensor')
- attention_entry_momentum: float32 [1024, 3, 1024], P('dp', None, 'tensor')
- attention_entry_variance: float32 [1024, 3, 1024], P('dp', None, 'tensor')
- attention_exit_gradient: float32 [1024, 1024], P('tensor', 'dp')
- attention_exit_updated: float32 [1024, 1024], P('tensor', 'dp')
- attention_exit_momentum: float32 [1024, 1024], P('tensor', 'dp')
- attention_exit_variance: float32 [1024, 1024], P('tensor', 'dp')
- feedforward_entry_gradient: float32 [1024, 2, 2624], P('dp', None, 'tensor')
- feedforward_entry_updated: float32 [1024, 2, 2624], P('dp', None, 'tensor')
- feedforward_entry_momentum: float32 [1024, 2, 2624], P('dp', None, 'tensor')
- feedforward_entry_variance: float32 [1024, 2, 2624], P('dp', None, 'tensor')
- feedforward_exit_gradient: float32 [2624, 1024], P('tensor', 'dp')
- feedforward_exit_updated: float32 [2624, 1024], P('tensor', 'dp')
- feedforward_exit_momentum: float32 [2624, 1024], P('tensor', 'dp')
- feedforward_exit_variance: float32 [2624, 1024], P('tensor', 'dp')
- norm_gains_gradient: float32 [2, 1024], P(None, 'dp')
- norm_gains_updated: float32 [2, 1024], P(None, 'dp')
- norm_gains_momentum: float32 [2, 1024], P(None, 'dp')
- norm_gains_variance: float32 [2, 1024], P(None, 'dp')
- update_norms: float32 [5, 2], replicated
The draws below stay inside these ranges and needn't reach their ends.
Inputs may be any that keep to these rules, and one draw needn't show every extreme that they name: `segment_ids`: each sequence of 1024 tokens is a pack of whole documents: its segment ids start at 0 at the sequence's first token and rise by one at each document's first token, so that a sequence of one-token documents reaches 1023. `positions`: counts from 0 at each document's first token and rises by one per token within the document; a document may fill a whole sequence.
All inputs are finite; a program needn't handle non-finite values.
Results may differ from the reference program's by a relative error of at most 0.012.
The reference program's roundings to bfloat16 on the way count: a program that leaves them out, or rounds other values in their place, can miss the bound.
Values may be sent and summed in bfloat16 or wider, within the bound.
No kernel may reach another device: no remote copies, remote signals or barrier semaphores. Data moves between devices by JAX's collectives and lax.ppermute only.
A program may use at most 192 MiB of HBM per device.

```python
import math
import jax
import jax.numpy as jnp
from jax import lax

D = 1024
HEADS = 16
HD = 64
FF = 2624
LEN = 1024
SEQS = 16
TOKENS = 16384


def document_layout(key):
    base_key = jax.random.fold_in(key, 11)
    level_key, tick_key, pick_key = jax.random.split(base_key, 3)
    sequences = TOKENS // LEN
    levels = jax.random.randint(level_key, (sequences, 1), 2, 10)
    limits = jnp.left_shift(jnp.ones_like(levels), levels)
    tick_values = jax.random.randint(tick_key, (sequences, LEN), 0, 1 << 20)
    column = jnp.arange(LEN, dtype=jnp.int32)[None, :]
    order = jax.random.permutation(pick_key, jnp.arange(sequences, dtype=jnp.int32))
    row_index = jnp.arange(sequences, dtype=jnp.int32)[:, None]
    whole_row = row_index == order[0]
    single_row = row_index == order[1]
    drawn_starts = jnp.logical_or(tick_values % limits == 0, column == 0)
    starts = jnp.where(whole_row, column == 0, jnp.where(single_row, True, drawn_starts))
    segment = jnp.cumsum(starts.astype(jnp.int32), axis=1) - 1
    first_index = lax.cummax(jnp.where(starts, column, 0), axis=1)
    return (segment.reshape(-1).astype(jnp.int32), (column - first_index).reshape(-1).astype(jnp.int32))


def draw_segment_ids(key, part):
    return document_layout(key)[0]


def draw_positions(key, part):
    return document_layout(key)[1]


def with_spikes(drawn, rng, source, target, blocks, factor):
    def block_of(axis_at):
        return (jnp.arange(drawn.shape[axis_at]) // (drawn.shape[axis_at] // blocks)).reshape((-1,) + (1,) * (drawn.ndim - 1 - axis_at))

    one_side = jax.random.permutation(rng, blocks)[block_of(target)]
    second = (block_of(target) + blocks // 2) % blocks
    return jnp.where((block_of(source) == one_side) | (block_of(source) == second), factor * drawn, drawn)


def steps_of(stream_key, dims, cuts, low, top_value):
    loudness = 1.0
    for dim, parts in cuts:
        heights = jax.random.uniform(jax.random.fold_in(jax.random.fold_in(stream_key, 6), dim), (parts,), jnp.float32, low / len(cuts), top_value / len(cuts))
        loudness = loudness * jnp.repeat(jnp.exp(heights), dims[dim] // parts).reshape((-1,) + (1,) * (len(dims) - 1 - dim))
    return loudness


def scatter_about(stream_key, dims, scale, reach, shards=(), kind=jnp.bfloat16):
    level = steps_of(stream_key, dims, shards, -0.22, 0.18) if shards else 1.0
    drawn = jax.random.normal(stream_key, dims, jnp.float32) * scale * level
    return jnp.minimum(jnp.maximum(drawn, -reach), reach).astype(kind)


def noise_with(rng, extent, width, bound, shards, heavy, held_as=jnp.bfloat16):
    result = width * jax.random.normal(rng, extent, jnp.float32)
    if shards:
        result = result * steps_of(rng, extent, shards, -0.22, 0.18)
    return jnp.clip(with_spikes(result, jax.random.fold_in(rng, 3), *heavy), -bound, bound).astype(held_as)


def setup_inputs(seed: int = 0) -> dict:
    key_list = jax.random.split(jax.random.key(seed), 20)
    tokens = scatter_about(key_list[0], (TOKENS, D), 1.0, 6.0, ((0, 32),))
    cotangent = noise_with(key_list[1], (TOKENS, D), 1.0, 6.0, ((0, 32),), (0, 1, 32, 2.75))
    segment_ids = draw_segment_ids(jax.random.fold_in(key_list[19], 71), 0)
    positions = draw_positions(jax.random.fold_in(key_list[19], 71), 0)
    attention_entry = scatter_about(key_list[4], (D, 3, D), D ** -0.5, 0.1875, ((0, 8), (2, 4)), jnp.float32)
    attention_exit = scatter_about(key_list[5], (D, D), (D // 4) ** -0.5, 0.375, ((0, 4), (1, 8)), jnp.float32)
    feedforward_entry = scatter_about(key_list[6], (D, 2, FF), D ** -0.5, 0.1875, ((0, 8), (2, 4)), jnp.float32)
    feedforward_exit = scatter_about(key_list[7], (FF, D), FF ** -0.5, 0.125, ((0, 4), (1, 8)), jnp.float32)
    norm_gains = jnp.clip(1.0 + 0.1 * jax.random.normal(key_list[8], (2, D), jnp.float32), 0.5, 1.5)
    momentum_attention_entry = scatter_about(key_list[9], (D, 3, D), (0.05 * TOKENS ** 0.5), 40.0, ((0, 8), (2, 4)), jnp.float32)
    momentum_attention_exit = scatter_about(key_list[10], (D, D), (0.05 * TOKENS ** 0.5), 40.0, ((0, 4), (1, 8)), jnp.float32)
    momentum_feedforward_entry = scatter_about(key_list[11], (D, 2, FF), (0.05 * TOKENS ** 0.5), 40.0, ((0, 8), (2, 4)), jnp.float32)
    momentum_feedforward_exit = scatter_about(key_list[12], (FF, D), (0.05 * TOKENS ** 0.5), 40.0, ((0, 4), (1, 8)), jnp.float32)
    momentum_norm_gains = scatter_about(key_list[13], (2, D), (0.05 * TOKENS ** 0.5), 40.0, ((1, 8),), jnp.float32)
    variance_attention_entry = jnp.clip(jnp.exp(math.log(819.2) - 3.218876 * jax.random.uniform(key_list[14], (D, 3, D), jnp.float32) ** steps_of(key_list[14], (D, 3, D), ((0, 8), (2, 4)), -0.2, 0.2)), 32.768, 819.2)
    variance_attention_exit = jnp.clip(jnp.exp(math.log(819.2) - 3.218876 * jax.random.uniform(key_list[15], (D, D), jnp.float32) ** steps_of(key_list[15], (D, D), ((0, 4), (1, 8)), -0.2, 0.2)), 32.768, 819.2)
    variance_feedforward_entry = jnp.clip(jnp.exp(math.log(819.2) - 3.218876 * jax.random.uniform(key_list[16], (D, 2, FF), jnp.float32) ** steps_of(key_list[16], (D, 2, FF), ((0, 8), (2, 4)), -0.2, 0.2)), 32.768, 819.2)
    variance_feedforward_exit = jnp.clip(jnp.exp(math.log(819.2) - 3.218876 * jax.random.uniform(key_list[17], (FF, D), jnp.float32) ** steps_of(key_list[17], (FF, D), ((0, 4), (1, 8)), -0.2, 0.2)), 32.768, 819.2)
    variance_norm_gains = jnp.clip(jnp.exp(math.log(819.2) - 3.218876 * jax.random.uniform(key_list[18], (2, D), jnp.float32) ** steps_of(key_list[18], (2, D), ((1, 8),), -0.2, 0.2)), 32.768, 819.2)
    return dict(tokens=tokens, cotangent=cotangent, segment_ids=segment_ids, positions=positions, attention_entry=attention_entry, attention_exit=attention_exit, feedforward_entry=feedforward_entry, feedforward_exit=feedforward_exit, norm_gains=norm_gains, momentum_attention_entry=momentum_attention_entry, momentum_attention_exit=momentum_attention_exit, momentum_feedforward_entry=momentum_feedforward_entry, momentum_feedforward_exit=momentum_feedforward_exit, momentum_norm_gains=momentum_norm_gains, variance_attention_entry=variance_attention_entry, variance_attention_exit=variance_attention_exit, variance_feedforward_entry=variance_feedforward_entry, variance_feedforward_exit=variance_feedforward_exit, variance_norm_gains=variance_norm_gains)


@jax.custom_vjp
def low(v):
    return lax.optimization_barrier(v.astype(jnp.bfloat16)).astype(jnp.float32)

@jax.custom_vjp
def low_back(v):
    return v

def low_keep(v):
    return (low(v), None)

def low_pass(kept, grad):
    return (grad,)

def back_keep(v):
    return (v, None)

def back_low(kept, grad):
    return (low(grad),)
low.defvjp(low_keep, low_pass)
low_back.defvjp(back_keep, back_low)
norm_eps = 1e-05
rope_base = 160000.0
masked_value = -1e+30
beta_one = 0.9
beta_two = 0.95
adam_eps = 1e-06
decay_rate = 0.01
learn_rate = 0.3
ratio_eps = 1e-06
highest = lax.Precision.HIGHEST

def matmul(first_arg, second_arg):
    return jnp.dot(first_arg, second_arg, precision=highest, preferred_element_type=jnp.float32)

def layer_norm(values, gain_row):
    center = values - lax.optimization_barrier(jnp.mean(values, axis=-1, keepdims=True))
    spread = lax.optimization_barrier(jnp.mean(center * center, axis=-1, keepdims=True))
    return center * lax.rsqrt(spread + norm_eps) * gain_row

def rope_tables(places):
    half_dim = HD // 2
    frequency = rope_base ** (-(jnp.arange(half_dim, dtype=jnp.float32) * 2.0 / HD))
    angles = places.astype(jnp.float32)[:, None] * frequency[None, :]
    cosine = jnp.concatenate([jnp.cos(angles), jnp.cos(angles)], axis=-1)[:, None, :]
    sine_table = jnp.concatenate([jnp.sin(angles), jnp.sin(angles)], axis=-1)[:, None, :]
    return (cosine, sine_table)

def rotary(values, cosine, sine_table):
    half_dim = values.shape[-1] // 2
    turned = jnp.concatenate([-values[..., half_dim:], values[..., :half_dim]], axis=-1)
    return values * cosine + turned * sine_table

def geglu(gate_part, up_part):
    return jax.nn.gelu(gate_part, approximate=False) * up_part

def sequence_forward(seq_tokens, segments, places, entry_low, exit_low, grow_low, shrink_low, gains_low):
    scale_factor = HD ** (-0.5)
    normed_one = low(layer_norm(seq_tokens, gains_low[0]))
    projected = low_back(matmul(normed_one, entry_low.reshape(D, 3 * D))).reshape(LEN, 3, HEADS, HD)
    cosine, sine_table = rope_tables(places)
    queries = low(rotary(projected[:, 0], cosine, sine_table))
    key_rows = low(rotary(projected[:, 1], cosine, sine_table))
    value_rows = low(projected[:, 2])
    scores = low_back(jnp.einsum('qhd,khd->hqk', queries, key_rows, precision=highest)) * scale_factor
    allowed = (segments[:, None] == segments[None, :])[None]
    scores = jnp.where(allowed, scores, masked_value)
    shifted = scores - lax.optimization_barrier(jnp.max(scores, axis=-1, keepdims=True))
    exp_scores = jnp.exp(shifted)
    probability = exp_scores / lax.optimization_barrier(jnp.sum(exp_scores, axis=-1, keepdims=True))
    mixed = jnp.einsum('hqk,khd->qhd', low(probability), value_rows, precision=highest)
    attended = low(low_back(mixed)).reshape(LEN, D)
    hidden_state = seq_tokens + low_back(matmul(attended, exit_low))
    normed_two = low(layer_norm(hidden_state, gains_low[1]))
    gate_up = low_back(matmul(normed_two, grow_low.reshape(D, 2 * FF))).reshape(LEN, 2, FF)
    activated = low(geglu(gate_up[:, 0], gate_up[:, 1]))
    return hidden_state + matmul(activated, shrink_low)

def group_size():
    per_group = max(1, min(SEQS, 2048 // LEN))
    while SEQS % per_group != 0:
        per_group = per_group - 1
    return per_group

def layer_forward(inputs, entry, leave, grow, shrink, gains, segment_ids, positions):
    entry_low = low(entry)
    exit_low = low(leave)
    grow_low = low(grow)
    shrink_low = low(shrink)
    gains_low = low(gains)
    per_group = group_size()
    groups = SEQS // per_group
    token_groups = inputs.reshape(groups, per_group, LEN, D)
    segment_groups = segment_ids.reshape(groups, per_group, LEN)
    place_groups = positions.reshape(groups, per_group, LEN)

    def one_sequence(seq_tokens, segments, places):
        return sequence_forward(seq_tokens, segments, places, entry_low, exit_low, grow_low, shrink_low, gains_low)

    def one_group(packed):
        part_tokens, part_segments, part_places = packed
        return jax.vmap(one_sequence)(part_tokens, part_segments, part_places)
    outputs = lax.map(jax.checkpoint(one_group), (token_groups, segment_groups, place_groups))
    return outputs.reshape(TOKENS, D)

def lamb(master, gradient, momentum, variance):
    new_momentum = beta_one * momentum + (1.0 - beta_one) * gradient
    new_variance = beta_two * variance + (1.0 - beta_two) * gradient * gradient
    update = new_momentum / (jnp.sqrt(new_variance) + adam_eps) + decay_rate * master
    weight_square = jnp.sum(master * master)
    update_square = jnp.sum(update * update)
    ratio = jnp.sqrt(weight_square / (update_square + ratio_eps))
    updated = master - learn_rate * ratio * update
    return (updated, new_momentum, new_variance, jnp.stack([jnp.sqrt(weight_square), jnp.sqrt(update_square)]))

def reference(tokens, cotangent, segment_ids, positions, attention_entry, attention_exit, feedforward_entry, feedforward_exit, norm_gains, momentum_attention_entry, momentum_attention_exit, momentum_feedforward_entry, momentum_feedforward_exit, momentum_norm_gains, variance_attention_entry, variance_attention_exit, variance_feedforward_entry, variance_feedforward_exit, variance_norm_gains):

    def wrapped(inputs, entry, leave, grow, shrink, gains):
        return layer_forward(inputs, entry, leave, grow, shrink, gains, segment_ids, positions)
    output, pullback = jax.vjp(wrapped, tokens.astype(jnp.float32), attention_entry, attention_exit, feedforward_entry, feedforward_exit, norm_gains)
    grads = pullback(cotangent.astype(jnp.float32))
    entry_new, entry_mom, entry_var, entry_norms = lamb(attention_entry, grads[1], momentum_attention_entry, variance_attention_entry)
    exit_new, exit_mom, exit_var, exit_norms = lamb(attention_exit, grads[2], momentum_attention_exit, variance_attention_exit)
    grow_new, grow_mom, grow_var, grow_norms = lamb(feedforward_entry, grads[3], momentum_feedforward_entry, variance_feedforward_entry)
    shrink_new, shrink_mom, shrink_var, shrink_norms = lamb(feedforward_exit, grads[4], momentum_feedforward_exit, variance_feedforward_exit)
    gains_new, gains_mom, gains_var, gains_norms = lamb(norm_gains, grads[5], momentum_norm_gains, variance_norm_gains)
    all_norms = jnp.stack([entry_norms, exit_norms, grow_norms, shrink_norms, gains_norms])
    return (output.astype(jnp.bfloat16), grads[0], grads[1], entry_new, entry_mom, entry_var, grads[2], exit_new, exit_mom, exit_var, grads[3], grow_new, grow_mom, grow_var, grads[4], shrink_new, shrink_mom, shrink_var, grads[5], gains_new, gains_mom, gains_var, all_norms)
```

```python
import jax
import jax.numpy as jnp
from jax import lax
from jax.experimental import pallas as pl
from jax.experimental.pallas import tpu as pltpu
from jax.sharding import PartitionSpec as P

HD = 64
LEN = 1024
HALF = HD // 2
PAIR = 2 * HD

norm_eps = 1e-05
rope_base = 160000.0
masked_value = -1e30
beta_one = 0.9
beta_two = 0.95
adam_eps = 1e-06
decay_rate = 0.01
learn_rate = 0.3
ratio_eps = 1e-06
score_scale = HD ** (-0.5)
root_half = 0.7071067811865476
root_two_pi = 0.3989422804014327

bf16 = jnp.bfloat16
f32 = jnp.float32
VMEM_LIMIT = 60 * 1024 * 1024


def dot_nn(a, b):
    return lax.dot_general(a, b, (((1,), (0,)), ((), ())), preferred_element_type=f32)


def dot_nt(a, b):
    return lax.dot_general(a, b, (((1,), (1,)), ((), ())), preferred_element_type=f32)


def dot_tn(a, b):
    return lax.dot_general(a, b, (((0,), (0,)), ((), ())), preferred_element_type=f32)


def exchange(value, axis, bit):
    size = lax.axis_size(axis)
    return lax.ppermute(value, axis, [(i, i ^ bit) for i in range(size)])


def swap_core(value):
    return exchange(value, "tensor", 1)


def upper_bits(size):
    return [1 << k for k in range(1, size.bit_length() - 1)]


def gather_stages(color):
    dp = lax.axis_size("dp")
    last = [("dp", 1), ("tensor", 2)]
    return [("dp", b) for b in upper_bits(dp)] + (last if color == 0 else last[::-1])


def gather_rows(part, color):
    held = part[None]
    for axis, bit in gather_stages(color):
        other = exchange(held, axis, bit)
        held = jnp.concatenate([held, other], axis=2 if axis == "dp" else 0)
    return held


def scatter_rows(full, color):
    held = full
    stages = gather_stages(color)[::-1]
    for index, (axis, bit) in enumerate(stages):
        if axis == "dp":
            half = held.shape[2] // 2
            keep, send = held[:, :, :half], held[:, :, half:]
        else:
            keep, send = held[:1], held[1:]
        got = exchange(send, axis, bit)
        held = keep.astype(f32) + got.astype(f32)
        if index < len(stages) - 1:
            held = held.astype(bf16)
    return held[0]


def relative_columns(value):
    dp = lax.axis_size("dp")
    rows, width = value.shape
    bits = dp.bit_length() - 1
    index = lax.axis_index("dp")
    cube = value.reshape((rows,) + (2,) * bits + (width // dp,))
    for k in range(bits):
        axis = 1 + (bits - 1 - k)
        cube = jnp.where((index >> k) & 1 == 1, jnp.flip(cube, axis), cube)
    order = (0, bits) + tuple(range(1, bits)) + (bits + 1,)
    return cube.transpose(order).reshape(rows, width)


def absolute_columns(value):
    dp = lax.axis_size("dp")
    rows, width = value.shape
    bits = dp.bit_length() - 1
    index = lax.axis_index("dp")
    cube = value.reshape((rows,) + (2,) * bits + (width // dp,))
    order = (0,) + tuple(range(2, bits + 1)) + (1, bits + 1)
    cube = cube.transpose(order)
    for k in range(bits):
        axis = 1 + (bits - 1 - k)
        cube = jnp.where((index >> k) & 1 == 1, jnp.flip(cube, axis), cube)
    return cube.reshape(rows, width)


def tree_sum(value, axis):
    size = lax.axis_size(axis)
    if size > 8:
        bit = 1
        while bit < size:
            value = value + exchange(value, axis, bit)
            bit *= 2
        return value
    terms = [value] + [exchange(value, axis, b) for b in range(1, size)]
    while len(terms) > 1:
        terms = [terms[i] + terms[i + 1] for i in range(0, len(terms), 2)]
    return terms[0]


def score_bias(segr_ref, segc_ref, bias_ref):
    bias_ref[...] = jnp.where(segc_ref[...] == segr_ref[...], 0.0, masked_value)


QB = 256


def attend_kernel(n1_ref, w_ref, cos_ref, sin_ref, segr_ref, segc_ref, qkv_ref, o_ref, lse_ref, bias_ref):
    @pl.when(pl.program_id(0) == 0)
    def _():
        score_bias(segr_ref, segc_ref, bias_ref)

    projected = dot_nt(w_ref[0], n1_ref[...])
    cosine, sine = cos_ref[...], sin_ref[...]

    def turned(rows):
        low, high = rows[:HALF], rows[HALF:]
        return jnp.concatenate([low * cosine - high * sine, high * cosine + low * sine], axis=0)

    for head in range(2):
        at = head * HD
        query = turned(projected[at : at + HD]).astype(bf16) * jnp.asarray(score_scale, bf16)
        key = turned(projected[PAIR + at : PAIR + at + HD])
        value = projected[2 * PAIR + at : 2 * PAIR + at + HD].astype(bf16)
        qkv_ref[0, at : at + HD] = query
        qkv_ref[0, PAIR + at : PAIR + at + HD] = key.astype(bf16)
        qkv_ref[0, 2 * PAIR + at : 2 * PAIR + at + HD] = value
        key_rows = key.T.astype(bf16)
        for block in range(LEN // QB):
            span = slice(block * QB, (block + 1) * QB)
            scores = dot_nn(key_rows, query[:, span]) + bias_ref[:, span]
            peak = jnp.max(scores, axis=0, keepdims=True)
            weight = jnp.exp(scores - peak)
            total = jnp.sum(weight, axis=0, keepdims=True)
            mixed = dot_nn(value, weight.astype(bf16)) / total
            o_ref[0, at : at + HD, span] = mixed.astype(bf16)
            lse_ref[0, head : head + 1, span] = peak + jnp.log(total)


def whole(shape):
    return pl.BlockSpec(shape, lambda i: (0,) * len(shape))


def leading(shape):
    return pl.BlockSpec((1,) + shape[1:], lambda i: (i,) + (0,) * (len(shape) - 1))


def attend(n1, w_entry, cosine, sine, seg_row, seg_col):
    pairs = w_entry.shape[0]
    width = n1.shape[1]
    return pl.pallas_call(
        attend_kernel,
        name="attend",
        grid=(pairs,),
        in_specs=[
            whole(n1.shape),
            leading(w_entry.shape),
            whole(cosine.shape),
            whole(sine.shape),
            whole(seg_row.shape),
            whole(seg_col.shape),
        ],
        out_specs=[
            leading((pairs, 3 * PAIR, LEN)),
            leading((pairs, PAIR, LEN)),
            leading((pairs, 2, LEN)),
        ],
        out_shape=[
            jax.ShapeDtypeStruct((pairs, 3 * PAIR, LEN), bf16),
            jax.ShapeDtypeStruct((pairs, PAIR, LEN), bf16),
            jax.ShapeDtypeStruct((pairs, 2, LEN), f32),
        ],
        scratch_shapes=[pltpu.VMEM((LEN, LEN), f32)],
        compiler_params=pltpu.CompilerParams(vmem_limit_bytes=VMEM_LIMIT),
        cost_estimate=pl.CostEstimate(
            flops=pairs * (2 * 3 * PAIR * width * LEN + 4 * 4 * PAIR * LEN * LEN),
            bytes_accessed=pairs * 4 * PAIR * LEN * 4,
            transcendentals=pairs * 2 * LEN * LEN,
        ),
    )(n1, w_entry, cosine, sine, seg_row, seg_col)


def attend_back_kernel(
    x_ref, dh_ref, qkv_ref, o_ref, lse_ref, cos_ref, sin_ref, segr_ref, segc_ref, dp_ref, bias_ref
):
    @pl.when(pl.program_id(0) == 0)
    def _():
        score_bias(segr_ref, segc_ref, bias_ref)

    cosine, sine = cos_ref[...], sin_ref[...]
    grad_mixed = dot_nt(x_ref[0], dh_ref[...]).astype(bf16)

    def turned_back(rows):
        low, high = rows[:HALF], rows[HALF:]
        return jnp.concatenate([low * cosine + high * sine, high * cosine - low * sine], axis=0)

    for head in range(2):
        at = head * HD
        query = qkv_ref[0, at : at + HD]
        key = qkv_ref[0, PAIR + at : PAIR + at + HD]
        value = qkv_ref[0, 2 * PAIR + at : 2 * PAIR + at + HD]
        grad_out = grad_mixed[at : at + HD]
        mixed = o_ref[0, at : at + HD].astype(f32)
        inner = jnp.sum(mixed * grad_out.astype(f32), axis=0, keepdims=True)
        key_rows = key.astype(f32).T.astype(bf16)
        value_rows = value.astype(f32).T.astype(bf16)
        query_grads = []
        key_grad = jnp.zeros((HD, LEN), f32)
        value_grad = jnp.zeros((HD, LEN), f32)
        for block in range(LEN // QB):
            span = slice(block * QB, (block + 1) * QB)
            scores = dot_nn(key_rows, query[:, span]) + bias_ref[:, span]
            weight = jnp.exp(scores - lse_ref[0, head : head + 1, span])
            grad_weight = dot_nn(value_rows, grad_out[:, span])
            grad_scores = (weight * (grad_weight - inner[:, span])).astype(bf16)
            query_grads.append(dot_nn(key, grad_scores))
            key_grad += dot_nt(query[:, span], grad_scores)
            value_grad += dot_nt(grad_out[:, span], weight.astype(bf16))
        query_grad = jnp.concatenate(query_grads, axis=1) * score_scale
        dp_ref[0, at : at + HD] = turned_back(query_grad).astype(bf16)
        dp_ref[0, PAIR + at : PAIR + at + HD] = turned_back(key_grad).astype(bf16)
        dp_ref[0, 2 * PAIR + at : 2 * PAIR + at + HD] = value_grad.astype(bf16)


def attend_back(w_exit, dh, qkv, mixed, lse, cosine, sine, seg_row, seg_col):
    pairs = w_exit.shape[0]
    width = dh.shape[1]
    return pl.pallas_call(
        attend_back_kernel,
        name="attend_back",
        grid=(pairs,),
        in_specs=[
            leading(w_exit.shape),
            whole(dh.shape),
            leading(qkv.shape),
            leading(mixed.shape),
            leading(lse.shape),
            whole(cosine.shape),
            whole(sine.shape),
            whole(seg_row.shape),
            whole(seg_col.shape),
        ],
        out_specs=leading(qkv.shape),
        out_shape=jax.ShapeDtypeStruct(qkv.shape, bf16),
        scratch_shapes=[pltpu.VMEM((LEN, LEN), f32)],
        compiler_params=pltpu.CompilerParams(vmem_limit_bytes=VMEM_LIMIT),
        cost_estimate=pl.CostEstimate(
            flops=pairs * (2 * PAIR * width * LEN + 10 * 4 * PAIR * LEN * LEN),
            bytes_accessed=pairs * 8 * PAIR * LEN * 2,
            transcendentals=pairs * 2 * LEN * LEN,
        ),
    )(w_exit, dh, qkv, mixed, lse, cosine, sine, seg_row, seg_col)


def row_spans(rows, most):
    pieces = -(-rows // most)
    step = -(-rows // pieces // 16) * 16
    return [(at, min(rows, at + step)) for at in range(0, rows, step)]


def feed_kernel(n2_ref, c_ref, w_ref, out_ref, dn_ref, dw_ref, out_acc, dn_acc):
    step = pl.program_id(0)

    @pl.when(step == 0)
    def _():
        out_acc[...] = jnp.zeros_like(out_acc)
        dn_acc[...] = jnp.zeros_like(dn_acc)

    hidden = w_ref.shape[2]
    n2, cot = n2_ref[...], c_ref[...]
    for lo, hi in row_spans(hidden, 336):
        w_gate, w_up, w_down = w_ref[0, 0, lo:hi], w_ref[0, 1, lo:hi], w_ref[0, 2, lo:hi]
        gate, up, grad_act = dot_nt(w_gate, n2), dot_nt(w_up, n2), dot_nt(w_down, cot)
        phi = 0.5 + 0.5 * lax.erf(gate * root_half)
        density = jnp.exp(-0.5 * gate * gate) * root_two_pi
        gelu = gate * phi
        active = (gelu * up).astype(bf16)
        grad_gate = (grad_act * up * (phi + gate * density)).astype(bf16)
        grad_up = (grad_act * gelu).astype(bf16)
        dw_ref[0, 0, lo:hi] = dot_nn(grad_gate, n2).astype(bf16)
        dw_ref[0, 1, lo:hi] = dot_nn(grad_up, n2).astype(bf16)
        dw_ref[0, 2, lo:hi] = dot_nn(active, cot).astype(bf16)
        out_acc[...] += dot_tn(active, w_down)
        dn_acc[...] += dot_tn(grad_gate, w_gate) + dot_tn(grad_up, w_up)

    @pl.when(step == pl.num_programs(0) - 1)
    def _():
        out_ref[...] = out_acc[...].astype(bf16)
        dn_ref[...] = dn_acc[...].astype(bf16)


def feed(n2, cot, weights):
    shape = n2.shape
    rows, width = shape
    hidden = weights.shape[2] * weights.shape[0]
    return pl.pallas_call(
        feed_kernel,
        name="feed",
        grid=(weights.shape[0],),
        in_specs=[whole(shape), whole(shape), leading(weights.shape)],
        out_specs=[whole(shape), whole(shape), leading(weights.shape)],
        out_shape=[
            jax.ShapeDtypeStruct(shape, bf16),
            jax.ShapeDtypeStruct(shape, bf16),
            jax.ShapeDtypeStruct(weights.shape, bf16),
        ],
        scratch_shapes=[pltpu.VMEM(shape, f32), pltpu.VMEM(shape, f32)],
        compiler_params=pltpu.CompilerParams(vmem_limit_bytes=VMEM_LIMIT),
        cost_estimate=pl.CostEstimate(
            flops=18 * rows * width * hidden,
            bytes_accessed=4 * rows * width * 2 + 12 * width * hidden,
            transcendentals=2 * rows * hidden,
        ),
    )(n2, cot, weights)


def norm_stats(values):
    center = values - jnp.mean(values, axis=-1, keepdims=True)
    spread = jnp.mean(center * center, axis=-1, keepdims=True)
    rate = lax.rsqrt(spread + norm_eps)
    return center * rate, rate


def norm_back(scaled, rate, gain, upstream):
    weighted = upstream * gain
    grad = rate * (
        weighted
        - jnp.mean(weighted, axis=-1, keepdims=True)
        - scaled * jnp.mean(weighted * scaled, axis=-1, keepdims=True)
    )
    return grad, jnp.sum(upstream * scaled, axis=0)


def rope_tables(places):
    frequency = rope_base ** (-(jnp.arange(HALF, dtype=f32) * 2.0 / HD))
    angles = frequency[:, None] * places.astype(f32)[None, :]
    return jnp.cos(angles), jnp.sin(angles)


def lamb_direction(master, gradient, momentum, variance):
    new_momentum = beta_one * momentum + (1.0 - beta_one) * gradient
    new_variance = beta_two * variance + (1.0 - beta_two) * gradient * gradient
    update = new_momentum / (jnp.sqrt(new_variance) + adam_eps) + decay_rate * master
    return (new_momentum, new_variance, update)


def per_device(
    tokens,
    cotangent,
    segment_ids,
    positions,
    attention_entry,
    attention_exit,
    feedforward_entry,
    feedforward_exit,
    norm_gains,
    momentum_attention_entry,
    momentum_attention_exit,
    momentum_feedforward_entry,
    momentum_feedforward_exit,
    momentum_norm_gains,
    variance_attention_entry,
    variance_attention_exit,
    variance_feedforward_entry,
    variance_feedforward_exit,
    variance_norm_gains,
):
    own, width = tokens.shape
    local = attention_entry.shape[0]
    slice_width = attention_exit.shape[0]
    hidden = feedforward_exit.shape[0]
    pairs = slice_width // PAIR
    tensor_size = lax.axis_size("tensor")
    assert tensor_size == 4 and own * 2 == LEN and segment_ids.shape[0] == 2 * LEN and pairs == 2

    entry_rows = (
        attention_entry.astype(bf16)
        .reshape(local, 3, pairs, PAIR)
        .transpose(2, 1, 3, 0)
        .reshape(pairs, 3 * PAIR, local)
    )
    exit_rows = attention_exit.astype(bf16).reshape(pairs, PAIR, local)
    feed_rows = jnp.concatenate(
        [
            feedforward_entry.astype(bf16).transpose(1, 2, 0).reshape(2 * hidden, local),
            feedforward_exit.astype(bf16),
        ],
        axis=0,
    )
    gains_held = norm_gains.astype(bf16)
    for axis, bit in gather_stages(0):
        if axis == "dp":
            gains_held = jnp.concatenate([gains_held, exchange(gains_held, axis, bit)], axis=1)
    gains = gains_held.astype(f32)

    w_entry = [gather_rows(entry_rows[p], p) for p in range(pairs)]
    w_exit = [gather_rows(exit_rows[p], p) for p in range(pairs)]
    spans = row_spans(3 * hidden, 512)
    w_feed = [gather_rows(feed_rows[lo:hi], k % 2) for k, (lo, hi) in enumerate(spans)]

    inputs = relative_columns(tokens).astype(f32)
    cot_own = relative_columns(cotangent)
    cot = jnp.concatenate([cot_own, swap_core(cot_own)], axis=0)
    lane = lax.axis_index("tensor")

    def rows_of(vector):
        first = lax.dynamic_slice_in_dim(vector, lane * own, own, 0)
        second = lax.dynamic_slice_in_dim(vector, (lane ^ 1) * own, own, 0)
        return jnp.concatenate([first, second])

    segments = rows_of(segment_ids)
    seg_row, seg_col = segments[None, :], segments[:, None]
    cosine, sine = rope_tables(rows_of(positions))

    scaled_one, rate_one = norm_stats(inputs)
    normed = (scaled_one * gains[0]).astype(bf16)
    n1 = jnp.concatenate([normed, swap_core(normed)], axis=0)
    entry_full = jnp.stack(w_entry, axis=1).reshape(2 * pairs, 3 * PAIR, width)
    exit_full = jnp.stack(w_exit, axis=1).reshape(2 * pairs, PAIR, width)
    qkv, mixed, lse = attend(n1, entry_full, cosine, sine, seg_row, seg_col)
    mixed_flat = mixed.reshape(2 * pairs * PAIR, LEN)
    branch = dot_tn(mixed_flat, exit_full.reshape(2 * pairs * PAIR, width))
    hidden_state = inputs + branch[:own] + swap_core(branch[own:].astype(bf16)).astype(f32)
    scaled_two, rate_two = norm_stats(hidden_state)
    normed_two = (scaled_two * gains[1]).astype(bf16)
    n2 = jnp.concatenate([normed_two, swap_core(normed_two)], axis=0)
    feed_full = jnp.concatenate(w_feed, axis=1).reshape(2, 3, hidden, width)
    out_part, dn_part, feed_grad = feed(n2, cot, feed_full)
    block_output = absolute_columns(
        (hidden_state + out_part[:own].astype(f32) + swap_core(out_part[own:]).astype(f32)).astype(bf16)
    )

    feed_flat = feed_grad.reshape(2, 3 * hidden, width)
    g_feed = [scatter_rows(feed_flat[:, lo:hi], k % 2) for k, (lo, hi) in enumerate(spans)]
    dn2 = dn_part[:own].astype(f32) + swap_core(dn_part[own:]).astype(f32)
    norm_grad, gain_two = norm_back(scaled_two, rate_two, gains[1], dn2)
    grad_hidden = cot_own.astype(f32) + norm_grad
    dh_own = grad_hidden.astype(bf16)
    dh = jnp.concatenate([dh_own, swap_core(dh_own)], axis=0)
    exit_grad = dot_nn(mixed_flat, dh).astype(bf16).reshape(2, pairs, PAIR, width)
    g_exit = [scatter_rows(exit_grad[:, p], p) for p in range(pairs)]
    dproj = attend_back(exit_full, dh, qkv, mixed, lse, cosine, sine, seg_row, seg_col)
    dproj_flat = dproj.reshape(2 * pairs * 3 * PAIR, LEN)
    entry_grad = dot_nn(dproj_flat, n1).astype(bf16).reshape(2, pairs, 3 * PAIR, width)
    g_entry = [scatter_rows(entry_grad[:, p], p) for p in range(pairs)]
    dn1_part = dot_tn(dproj_flat, entry_full.reshape(2 * pairs * 3 * PAIR, width))
    dn1 = dn1_part[:own] + swap_core(dn1_part[own:].astype(bf16)).astype(f32)
    norm_grad_one, gain_one = norm_back(scaled_one, rate_one, gains[0], dn1)
    input_gradient = absolute_columns(grad_hidden + norm_grad_one)

    gains_local = jnp.stack([gain_one, gain_two])
    for axis, bit in gather_stages(0)[::-1]:
        if axis == "dp":
            half = gains_local.shape[1] // 2
            gains_local = gains_local[:, :half] + exchange(gains_local[:, half:], axis, bit)
    gains_gradient = tree_sum(gains_local, "tensor")
    entry_gradient = (
        jnp.stack(g_entry).reshape(pairs, 3, PAIR, local).transpose(3, 1, 0, 2).reshape(local, 3, slice_width)
    )
    exit_gradient = jnp.concatenate(g_exit, axis=0)
    feed_gradient = jnp.concatenate(g_feed, axis=0)
    grow_gradient = feed_gradient[: 2 * hidden].reshape(2, hidden, local).transpose(2, 0, 1)
    shrink_gradient = feed_gradient[2 * hidden :]
    gradients = (entry_gradient, exit_gradient, grow_gradient, shrink_gradient, gains_gradient)

    masters = (attention_entry, attention_exit, feedforward_entry, feedforward_exit, norm_gains)
    momenta = (
        momentum_attention_entry,
        momentum_attention_exit,
        momentum_feedforward_entry,
        momentum_feedforward_exit,
        momentum_norm_gains,
    )
    variances = (
        variance_attention_entry,
        variance_attention_exit,
        variance_feedforward_entry,
        variance_feedforward_exit,
        variance_norm_gains,
    )
    first_tensor = (lane == 0).astype(f32)
    shares = (1.0, 1.0, 1.0, 1.0, first_tensor)
    states = []
    square_rows = []
    for master, gradient, momentum, variance, share in zip(masters, gradients, momenta, variances, shares):
        new_momentum, new_variance, update = lamb_direction(master, gradient, momentum, variance)
        states.append((new_momentum, new_variance, update))
        square_rows.append(jnp.stack([jnp.sum(master * master), jnp.sum(update * update)]) * share)
    totals = tree_sum(tree_sum(jnp.stack(square_rows), "tensor"), "dp")
    updated_all = []
    for index in range(5):
        ratio = jnp.sqrt(totals[index, 0] / (totals[index, 1] + ratio_eps))
        updated_all.append(masters[index] - learn_rate * ratio * states[index][2])
    outputs = [block_output, input_gradient]
    for index in range(5):
        outputs += [gradients[index], updated_all[index], states[index][0], states[index][1]]
    return tuple(outputs + [jnp.sqrt(totals)])


def solution(mesh):
    rows = P(("dp", "tensor"), None)
    first = P("dp", None, "tensor")
    second = P("tensor", "dp")
    gains = P(None, "dp")
    weights = (first, second, first, second, gains)
    in_specs = (rows, rows, P("dp"), P("dp")) + weights * 3
    out_specs = (rows, rows) + tuple(spec for spec in weights for _ in range(4)) + (P(),)
    return jax.shard_map(per_device, mesh=mesh, in_specs=in_specs, out_specs=out_specs, check_vma=False)
```

```python
import jax
import jax.numpy as jnp
from jax import lax
from jax.experimental import pallas as pl
from jax.experimental.pallas import tpu as pltpu
from jax.sharding import PartitionSpec as P

HD = 64
LEN = 1024
HALF = HD // 2
PAIR = 2 * HD

norm_eps = 1e-05
rope_base = 160000.0
masked_value = -1e30
beta_one = 0.9
beta_two = 0.95
adam_eps = 1e-06
decay_rate = 0.01
learn_rate = 0.3
ratio_eps = 1e-06
score_scale = HD ** (-0.5)
root_half = 0.7071067811865476
root_two_pi = 0.3989422804014327

bf16 = jnp.bfloat16
f32 = jnp.float32
VMEM_LIMIT = 60 * 1024 * 1024


def dot_nn(a, b):
    return lax.dot_general(a, b, (((1,), (0,)), ((), ())), preferred_element_type=f32)


def dot_nt(a, b):
    return lax.dot_general(a, b, (((1,), (1,)), ((), ())), preferred_element_type=f32)


def dot_tn(a, b):
    return lax.dot_general(a, b, (((0,), (0,)), ((), ())), preferred_element_type=f32)


def exchange(value, axis, bit, *first):
    if first:
        value = lax.optimization_barrier((value,) + first)[0]
    size = lax.axis_size(axis)
    return lax.ppermute(value, axis, [(i, i ^ bit) for i in range(size)])


def swap_core(value):
    return exchange(value, "tensor", 1)


def upper_bits(size):
    return [1 << k for k in range(size.bit_length() - 2, 0, -1)]


def lanes(*parts):
    return jnp.concatenate(parts, axis=-1)


def add(keep, got):
    return (keep.astype(f32) + got.astype(f32)).astype(bf16)


def reversed_bits(value, bits):
    out = 0
    for k in range(bits):
        out = out + (((value >> k) & 1) << (bits - 1 - k))
    return out


def column_blocks(width):
    dp = lax.axis_size("dp")
    if (width // dp) % 128:
        return width, jnp.zeros((1,), jnp.int32)
    bits = dp.bit_length() - 1
    places = jnp.stack([lax.axis_index("dp") ^ reversed_bits(p, bits) for p in range(dp)])
    return width // dp, places.astype(jnp.int32)


def flip_columns(value, back):
    dp = lax.axis_size("dp")
    rows, width = value.shape
    if (width // dp) % 128 == 0:
        return value
    bits = dp.bit_length() - 1
    index = lax.axis_index("dp")
    order = (0,) + tuple(range(bits, 0, -1)) + (bits + 1,)
    cube = value.reshape((rows,) + (2,) * bits + (width // dp,))
    if back:
        cube = cube.transpose(order)
    for k in range(bits):
        axis = bits - k
        cube = jnp.where((index >> k) & 1 == 1, jnp.flip(cube, axis), cube)
    if not back:
        cube = cube.transpose(order)
    return cube.reshape(rows, width)


def tree_sum(value, axis):
    bit = 1
    while bit < lax.axis_size(axis):
        value = value + exchange(value, axis, bit)
        bit *= 2
    return value


def call(kernel, name, grid, in_specs, out_specs, out_shape, scratch, cost, scalars=0):
    return pl.pallas_call(
        kernel,
        name=name,
        grid_spec=pltpu.PrefetchScalarGridSpec(
            num_scalar_prefetch=scalars,
            grid=grid,
            in_specs=in_specs,
            out_specs=out_specs,
            scratch_shapes=scratch,
        ),
        out_shape=out_shape,
        compiler_params=pltpu.CompilerParams(vmem_limit_bytes=VMEM_LIMIT),
        cost_estimate=pl.CostEstimate(flops=cost[0], bytes_accessed=cost[1], transcendentals=cost[2]),
    )


def whole(shape):
    return pl.BlockSpec(shape, lambda i, *_: (0,) * len(shape))


def leading(shape):
    return pl.BlockSpec((1,) + shape[1:], lambda i, *_: (i,) + (0,) * (len(shape) - 1))


def banded(shape, rows):
    return pl.BlockSpec((rows,) + shape[1:], lambda i, *_: (i,) + (0,) * (len(shape) - 1))


def like(shape, dtype):
    return jax.ShapeDtypeStruct(shape, dtype)


def join(full_ref, own_ref, other_ref):
    half = own_ref.shape[0]
    full_ref[:half] = own_ref[...]
    full_ref[half:] = other_ref[...]


ROWS = 256


def norm_stats(values):
    center = values - jnp.mean(values, axis=-1, keepdims=True)
    spread = jnp.mean(center * center, axis=-1, keepdims=True)
    rate = lax.rsqrt(spread + norm_eps)
    return center * rate, rate


def norm_back(scaled, rate, gain, upstream):
    weighted = upstream * gain
    grad = rate * (
        weighted
        - jnp.mean(weighted, axis=-1, keepdims=True)
        - scaled * jnp.mean(weighted * scaled, axis=-1, keepdims=True)
    )
    return grad, jnp.sum(upstream * scaled, axis=0, keepdims=True)


def enter_kernel(block, places_ref, tokens_ref, cot_ref, gains_ref, x_ref, c_ref, n_ref):
    width = tokens_ref.shape[1]
    for p in range(width // block):
        source = pl.ds(pl.multiple_of(places_ref[p] * block, 128), block)
        target = slice(p * block, (p + 1) * block)
        x_ref[:, target] = tokens_ref[:, source]
        c_ref[:, target] = cot_ref[:, source]
    scaled, _ = norm_stats(x_ref[...].astype(f32))
    n_ref[...] = (scaled * gains_ref[0:1]).astype(bf16)


def enter(block, places, tokens, cotangent, gains):
    shape = tokens.shape
    spec = banded(shape, ROWS)
    return call(
        lambda *refs: enter_kernel(block, *refs),
        "enter",
        (shape[0] // ROWS,),
        [spec, spec, whole(gains.shape)],
        [spec] * 3,
        [like(shape, bf16)] * 3,
        [],
        (20 * shape[0] * shape[1], 10 * shape[0] * shape[1], 0),
        scalars=1,
    )(places, tokens, cotangent, gains)


def branch_kernel(mixed_refs, x_ref, own_ref, send_ref):
    step = pl.program_id(0)
    half = own_ref.shape[0]
    pieces = [(mixed_refs[0], 0, 0, 0), (mixed_refs[1], 0, 1, 0), (mixed_refs[2], 0, 0, 1), (mixed_refs[2], 1, 1, 1)]
    rows = jnp.concatenate([ref[i] for ref, i, _, _ in pieces], axis=0)
    weights = jnp.concatenate([x_ref[x, p * PAIR : (p + 1) * PAIR] for _, _, x, p in pieces], axis=0)
    total = dot_tn(rows, weights)

    @pl.when(step == 0)
    def _():
        own_ref[...] = total

    @pl.when(step == 1)
    def _():
        send_ref[...] = total.astype(bf16)


def branch(mixed, weights, pairs):
    own, width = LEN // 2, weights.shape[2]
    half_lanes = [pl.BlockSpec(m.shape[:2] + (own,), lambda i, *_: (0, 0, i)) for m in mixed]
    return call(
        lambda a, b, c, *refs: branch_kernel((a, b, c), *refs),
        "branch",
        (2,),
        half_lanes + [pl.BlockSpec((2, pairs * PAIR, width), lambda i, *_: (0, 0, 0))],
        [whole((own, width))] * 2,
        [like((own, width), f32), like((own, width), bf16)],
        [],
        (2 * LEN * width * 2 * pairs * PAIR, 8 * LEN * width, 0),
    )(*mixed, weights)


def middle_kernel(x_ref, part_ref, got_ref, gains_ref, h_ref, n_ref):
    hidden = x_ref[...].astype(f32) + part_ref[...] + got_ref[...].astype(f32)
    h_ref[...] = hidden
    scaled, _ = norm_stats(hidden)
    n_ref[...] = (scaled * gains_ref[1:2]).astype(bf16)


def middle(x, part, got, gains):
    shape = x.shape
    spec = banded(shape, ROWS)
    return call(
        middle_kernel,
        "middle",
        (shape[0] // ROWS,),
        [spec] * 3 + [whole(gains.shape)],
        [spec] * 2,
        [like(shape, f32), like(shape, bf16)],
        [],
        (20 * shape[0] * shape[1], 14 * shape[0] * shape[1], 0),
    )(x, part, got, gains)


def turn_kernel(h_ref, part_ref, got_ref, c_ref, gains_ref, dh_ref, low_ref, gain_ref):
    scaled, rate = norm_stats(h_ref[...])
    upstream = part_ref[...].astype(f32) + got_ref[...].astype(f32)
    grad, gain_grad = norm_back(scaled, rate, gains_ref[1:2], upstream)
    total = c_ref[...].astype(f32) + grad
    dh_ref[...] = total
    low_ref[...] = total.astype(bf16)

    @pl.when(pl.program_id(0) == 0)
    def _():
        gain_ref[...] = gain_grad

    @pl.when(pl.program_id(0) > 0)
    def _():
        gain_ref[...] += gain_grad


def turn(h, part, got, c, gains):
    shape = h.shape
    spec = banded(shape, ROWS)
    return call(
        turn_kernel,
        "turn",
        (shape[0] // ROWS,),
        [spec] * 4 + [whole(gains.shape)],
        [spec, spec, whole((1, shape[1]))],
        [like(shape, f32), like(shape, bf16), like((1, shape[1]), f32)],
        [],
        (30 * shape[0] * shape[1], 16 * shape[0] * shape[1], 0),
    )(h, part, got, c, gains)


def result_kernel(block, places_ref, h_ref, part_ref, got_ref, out_ref):
    for p in range(h_ref.shape[1] // block):
        source = slice(p * block, (p + 1) * block)
        target = pl.ds(pl.multiple_of(places_ref[p] * block, 128), block)
        total = h_ref[:, source] + part_ref[:, source].astype(f32) + got_ref[:, source].astype(f32)
        out_ref[:, target] = total.astype(bf16)


def result(block, places, h, part, got):
    shape = h.shape
    spec = banded(shape, ROWS)
    return call(
        lambda *refs: result_kernel(block, *refs),
        "result",
        (shape[0] // ROWS,),
        [spec] * 3,
        spec,
        like(shape, bf16),
        [],
        (3 * shape[0] * shape[1], 10 * shape[0] * shape[1], 0),
        scalars=1,
    )(places, h, part, got)


def leave_kernel(block, places_ref, x_ref, part_ref, got_ref, dh_ref, gains_ref, out_ref, gain_ref):
    scaled, rate = norm_stats(x_ref[...].astype(f32))
    upstream = part_ref[...].astype(f32) + got_ref[...].astype(f32)
    grad, gain_grad = norm_back(scaled, rate, gains_ref[0:1], upstream)
    total = dh_ref[...] + grad
    for p in range(x_ref.shape[1] // block):
        target = pl.ds(pl.multiple_of(places_ref[p] * block, 128), block)
        out_ref[:, target] = total[:, p * block : (p + 1) * block]

    @pl.when(pl.program_id(0) == 0)
    def _():
        gain_ref[...] = gain_grad

    @pl.when(pl.program_id(0) > 0)
    def _():
        gain_ref[...] += gain_grad


def leave(block, places, x, part, got, dh, gains):
    shape = x.shape
    spec = banded(shape, ROWS)
    return call(
        lambda *refs: leave_kernel(block, *refs),
        "leave",
        (shape[0] // ROWS,),
        [spec] * 4 + [whole(gains.shape)],
        [spec, whole((1, shape[1]))],
        [like(shape, f32), like((1, shape[1]), f32)],
        [],
        (30 * shape[0] * shape[1], 16 * shape[0] * shape[1], 0),
        scalars=1,
    )(places, x, part, got, dh, gains)


def last_kernel(dp_refs, w_refs, own_ref, send_ref):
    step = pl.program_id(0)
    total = None
    for dp_ref, w_ref in zip(dp_refs, w_refs):
        for i in range(dp_ref.shape[0]):
            term = dot_tn(dp_ref[i], w_ref[i])
            total = term if total is None else total + term

    @pl.when(step == 0)
    def _():
        send_ref[...] = total.astype(bf16)

    @pl.when(step == 1)
    def _():
        own_ref[...] = total


def last(dproj, weights):
    own, width = LEN // 2, weights[0].shape[2]
    count = len(dproj)
    half_lanes = [pl.BlockSpec(d.shape[:2] + (own,), lambda i, *_: (0, 0, 1 - i)) for d in dproj]
    rows = sum(d.shape[0] * d.shape[1] for d in dproj)
    return call(
        lambda *refs: last_kernel(refs[:count], refs[count : 2 * count], *refs[2 * count :]),
        "last",
        (2,),
        half_lanes + [whole(w.shape) for w in weights],
        [whole((own, width))] * 2,
        [like((own, width), f32), like((own, width), bf16)],
        [],
        (2 * LEN * width * rows, 4 * rows * LEN + 6 * LEN * width, 0),
    )(*dproj, *weights)


QB = 256


def score_bias(segr_ref, segc_ref, bias_ref):
    bias_ref[...] = jnp.where(segc_ref[...] == segr_ref[...], 0.0, masked_value)


def attend_kernel(
    own_ref, other_ref, w_ref, cos_ref, sin_ref, segr_ref, segc_ref, qkv_ref, o_ref, lse_ref, bias_ref, n_ref, key_ref
):
    @pl.when(pl.program_id(0) == 0)
    def _():
        score_bias(segr_ref, segc_ref, bias_ref)
        join(n_ref, own_ref, other_ref)

    projected = dot_nt(w_ref[0], n_ref[...])
    cosine, sine = cos_ref[...], sin_ref[...]

    def turned(rows):
        low, high = rows[:HALF], rows[HALF:]
        return jnp.concatenate([low * cosine - high * sine, high * cosine + low * sine], axis=0)

    for head in range(2):
        at = head * HD
        query = turned(projected[at : at + HD]).astype(bf16) * jnp.asarray(score_scale, bf16)
        key = turned(projected[PAIR + at : PAIR + at + HD])
        qkv_ref[0, at : at + HD] = query
        qkv_ref[0, PAIR + at : PAIR + at + HD] = key.astype(bf16)
        qkv_ref[0, 2 * PAIR + at : 2 * PAIR + at + HD] = projected[2 * PAIR + at : 2 * PAIR + at + HD].astype(bf16)
        key_ref[head] = key.T.astype(bf16)

    @pl.loop(0, LEN // QB)
    def _(block):
        span = pl.ds(pl.multiple_of(block * QB, QB), QB)
        for head in range(2):
            at = head * HD
            query = qkv_ref[0, at : at + HD, span]
            value = qkv_ref[0, 2 * PAIR + at : 2 * PAIR + at + HD]
            scores = dot_nn(key_ref[head], query) + bias_ref[:, span]
            peak = jnp.max(scores, axis=0, keepdims=True)
            weight = jnp.exp(scores - peak)
            total = jnp.sum(weight, axis=0, keepdims=True)
            mixed = dot_nn(value, weight.astype(bf16)) / total
            o_ref[0, at : at + HD, span] = mixed.astype(bf16)
            lse_ref[0, head : head + 1, span] = peak + jnp.log(total)


def attend(own, other, weights, tables):
    pairs = weights.shape[0]
    width = own.shape[1]
    return call(
        attend_kernel,
        "attend",
        (pairs,),
        [whole(own.shape), whole(other.shape), leading(weights.shape)] + [whole(t.shape) for t in tables],
        [leading((pairs, 3 * PAIR, LEN)), leading((pairs, PAIR, LEN)), leading((pairs, 2, LEN))],
        [like((pairs, 3 * PAIR, LEN), bf16), like((pairs, PAIR, LEN), bf16), like((pairs, 2, LEN), f32)],
        [pltpu.VMEM((LEN, LEN), f32), pltpu.VMEM((LEN, width), bf16), pltpu.VMEM((2, LEN, HD), bf16)],
        (pairs * (6 * PAIR * width * LEN + 16 * PAIR * LEN * LEN), pairs * 16 * PAIR * LEN, pairs * 2 * LEN * LEN),
    )(own, other, weights, *tables)


def attend_back_kernel(
    n_own, n_other, dh_own, dh_other, x_ref, qkv_ref, o_ref, lse_ref, cos_ref, sin_ref, segr_ref, segc_ref,
    dp_ref, low_ref, high_ref, bias_ref, n_ref, dh_ref, rows_ref, do_ref, inner_ref, grad_ref,
):
    @pl.when(pl.program_id(0) == 0)
    def _():
        score_bias(segr_ref, segc_ref, bias_ref)
        join(n_ref, n_own, n_other)
        join(dh_ref, dh_own, dh_other)

    cosine, sine = cos_ref[...], sin_ref[...]
    do_ref[...] = dot_nt(x_ref[0], dh_ref[...]).astype(bf16)
    for head in range(2):
        at = head * HD
        mixed = o_ref[0, at : at + HD].astype(f32)
        inner_ref[head : head + 1] = jnp.sum(mixed * do_ref[at : at + HD].astype(f32), axis=0, keepdims=True)
        rows_ref[head] = qkv_ref[0, PAIR + at : PAIR + at + HD].astype(f32).T.astype(bf16)
        rows_ref[2 + head] = qkv_ref[0, 2 * PAIR + at : 2 * PAIR + at + HD].astype(f32).T.astype(bf16)
    grad_ref[...] = jnp.zeros_like(grad_ref)

    @pl.loop(0, LEN // QB)
    def _(block):
        span = pl.ds(pl.multiple_of(block * QB, QB), QB)
        for head in range(2):
            at = head * HD
            query = qkv_ref[0, at : at + HD, span]
            key = qkv_ref[0, PAIR + at : PAIR + at + HD]
            grad_out = do_ref[at : at + HD, span]
            scores = dot_nn(rows_ref[head], query) + bias_ref[:, span]
            weight = jnp.exp(scores - lse_ref[0, head : head + 1, span])
            grad_weight = dot_nn(rows_ref[2 + head], grad_out)
            grad_scores = (weight * (grad_weight - inner_ref[head : head + 1, span])).astype(bf16)
            grad_ref[at : at + HD, span] = dot_nn(key, grad_scores) * score_scale
            grad_ref[PAIR + at : PAIR + at + HD] += dot_nt(query, grad_scores)
            grad_ref[2 * PAIR + at : 2 * PAIR + at + HD] += dot_nt(grad_out, weight.astype(bf16))

    for at in range(0, 2 * PAIR, HD):
        low, high = grad_ref[at : at + HALF], grad_ref[at + HALF : at + HD]
        dp_ref[0, at : at + HALF] = (low * cosine + high * sine).astype(bf16)
        dp_ref[0, at + HALF : at + HD] = (high * cosine - low * sine).astype(bf16)
    dp_ref[0, 2 * PAIR :] = grad_ref[2 * PAIR :].astype(bf16)
    half = low_ref.shape[2]
    for ref, cut in ((low_ref, slice(0, half)), (high_ref, slice(half, 2 * half))):
        ref[0, : 3 * PAIR] = dot_nn(dp_ref[0], n_ref[:, cut]).astype(bf16)
        ref[0, 3 * PAIR :] = dot_nn(o_ref[0], dh_ref[:, cut]).astype(bf16)


def attend_back(rows, grads, weights, place, qkv, mixed, lse, tables):
    pairs = qkv.shape[0]
    width = rows[0].shape[1]
    half = (pairs, 4 * PAIR, width // 2)
    return call(
        attend_back_kernel,
        "attend_back",
        (pairs,),
        [whole(rows[0].shape)] * 4
        + [pl.BlockSpec((1, PAIR, width), lambda i, *_: place(i) + (0,))]
        + [leading(qkv.shape), leading(mixed.shape), leading(lse.shape)]
        + [whole(t.shape) for t in tables],
        [leading(qkv.shape), leading(half), leading(half)],
        [like(qkv.shape, bf16), like(half, bf16), like(half, bf16)],
        [
            pltpu.VMEM((LEN, LEN), f32),
            pltpu.VMEM((LEN, width), bf16),
            pltpu.VMEM((LEN, width), bf16),
            pltpu.VMEM((4, LEN, HD), bf16),
            pltpu.VMEM((PAIR, LEN), bf16),
            pltpu.VMEM((2, LEN), f32),
            pltpu.VMEM((3 * PAIR, LEN), f32),
        ],
        (
            pairs * (10 * PAIR * width * LEN + 40 * PAIR * LEN * LEN),
            pairs * 40 * PAIR * LEN,
            pairs * 2 * LEN * LEN,
        ),
    )(*rows, *grads, weights, qkv, mixed, lse, *tables)


def take(refs, plan, name):
    found = []
    for ref, segments in zip(refs, plan):
        at = 0
        for label, lo, hi in segments:
            if label == name:
                found.append((lo, ref[0, at : at + hi - lo]))
            at += hi - lo
    found = [rows for _, rows in sorted(found, key=lambda f: f[0])]
    return found[0] if len(found) == 1 else jnp.concatenate(found, axis=0)


def put(stores, plan, name, value):
    for store, segments in zip(stores, plan):
        at = 0
        for label, lo, hi in segments:
            if label == name:
                store(slice(at, at + hi - lo), value[lo:hi])
            at += hi - lo


def feed_kernel(plan, grad_plan, first, refs):
    n_own, n_other, c_own, c_other, wa_ref, wb_ref = refs[:6]
    refs = refs[6:]
    if not first:
        out_in, dn_in = refs[:2]
        refs = refs[2:]
    out_refs, ga_ref, low_ref, high_ref, n_ref, c_ref, out_acc, dn_acc = refs[:-7], *refs[-7:]
    step = pl.program_id(0)

    @pl.when(step == 0)
    def _():
        join(n_ref, n_own, n_other)
        join(c_ref, c_own, c_other)
        out_acc[...] = jnp.zeros_like(out_acc) if first else out_in[...]
        dn_acc[...] = jnp.zeros_like(dn_acc) if first else dn_in[...]

    n2, cot = n_ref[...], c_ref[...]
    weights = (wa_ref, wb_ref)
    w_gate, w_up, w_down = (take(weights, plan, name) for name in "abf")
    gate, up, grad_act = dot_nt(w_gate, n2), dot_nt(w_up, n2), dot_nt(w_down, cot)
    phi = 0.5 + 0.5 * lax.erf(gate * root_half)
    density = jnp.exp(-0.5 * gate * gate) * root_two_pi
    gelu = gate * phi
    active = (gelu * up).astype(bf16)
    grad_gate = (grad_act * up * (phi + gate * density)).astype(bf16)
    grad_up = (grad_act * gelu).astype(bf16)

    def store_a(rows, value):
        ga_ref[0, rows] = value

    def store_b(rows, value):
        half = low_ref.shape[2]
        low_ref[0, rows] = value[:, :half]
        high_ref[0, rows] = value[:, half:]

    for name, left, right in (("a", grad_gate, n2), ("b", grad_up, n2), ("f", active, cot)):
        put((store_a, store_b), grad_plan, name, dot_nn(left, right).astype(bf16))
    out_acc[...] += dot_tn(active, w_down)
    dn_acc[...] += dot_tn(grad_gate, w_gate) + dot_tn(grad_up, w_up)

    @pl.when(step == pl.num_programs(0) - 1)
    def _():
        if first:
            out_refs[0][...] = out_acc[...]
            out_refs[1][...] = dn_acc[...]
        else:
            half = out_refs[0].shape[0]
            out_refs[0][...] = out_acc[:half].astype(bf16)
            out_refs[1][...] = out_acc[half:].astype(bf16)
            out_refs[2][...] = dn_acc[:half].astype(bf16)
            out_refs[3][...] = dn_acc[half:].astype(bf16)


def length(segments):
    return sum(hi - lo for _, lo, hi in segments)


def feed(n2, cot, weights, sums, plan, grad_plan):
    own, width = n2[0].shape
    first = not sums
    count = weights[0].shape[0]
    ga = (count, length(grad_plan[0]), width)
    gb = (count, length(grad_plan[1]), width // 2)
    hidden = sum(hi - lo for segments in plan for name, lo, hi in segments if name == "a")
    full, half = (LEN, width), (own, width)
    outs = [like(full, f32)] * 2 if first else [like(half, bf16)] * 4
    return call(
        lambda *refs: feed_kernel(plan, grad_plan, first, refs),
        "feed",
        (count,),
        [whole(half)] * 4 + [leading(w.shape) for w in weights] + [whole(full)] * len(sums),
        [whole(o.shape) for o in outs] + [leading(ga), leading(gb), leading(gb)],
        outs + [like(ga, bf16), like(gb, bf16), like(gb, bf16)],
        [pltpu.VMEM(full, bf16), pltpu.VMEM(full, bf16), pltpu.VMEM(full, f32), pltpu.VMEM(full, f32)],
        (18 * LEN * width * count * hidden, 16 * LEN * width + 12 * width * count * hidden, 2 * LEN * count * hidden),
    )(*n2, *cot, *weights, *sums)


def rope_tables(places):
    frequency = rope_base ** (-(jnp.arange(HALF, dtype=f32) * 2.0 / HD))
    angles = frequency[:, None] * places.astype(f32)[None, :]
    return jnp.cos(angles), jnp.sin(angles)


def lamb_direction(master, gradient, momentum, variance):
    new_momentum = beta_one * momentum + (1.0 - beta_one) * gradient
    new_variance = beta_two * variance + (1.0 - beta_two) * gradient * gradient
    update = new_momentum / (jnp.sqrt(new_variance) + adam_eps) + decay_rate * master
    return (new_momentum, new_variance, update)


class Gather:
    def __init__(self, rows, split):
        self.held, self.split = rows, split

    def hop(self, bit, *first):
        got = exchange(self.held, "dp", bit, *first)
        self.held = lanes(self.held, got)
        return got

    def cross(self, *first):
        a, b = self.held[: self.split], self.held[self.split :]
        got_a = exchange(a, "dp", 1, *first)
        got_b = exchange(b, "tensor", 2, *first)
        self.a = lanes(a, got_a)
        self.b = jnp.stack([b, got_b])
        return got_a, got_b

    def finish(self, *first):
        got_a = exchange(self.a, "tensor", 2, *first)
        got_b = exchange(self.b, "dp", 1, *first)
        self.other_a = got_a
        self.b = lanes(self.b, got_b)
        return got_a, got_b

    def arrays(self):
        return jnp.stack([self.a, self.other_a]), self.b


class Scatter:
    def __init__(self, keep_a, send_a, low_b, high_b):
        self.keep_a, self.send_a, self.low_b, self.high_b = keep_a, send_a, low_b, high_b

    def start(self, *first):
        got_a = exchange(self.send_a, "tensor", 2, *first)
        got_b = exchange(self.high_b, "dp", 1, *first)
        self.a, self.b = add(self.keep_a, got_a), add(self.low_b, got_b)
        return got_a, got_b

    def cross(self, *first):
        half = self.a.shape[-1] // 2
        got_a = exchange(self.a[:, half:], "dp", 1, *first)
        got_b = exchange(self.b[1], "tensor", 2, *first)
        self.held = jnp.concatenate([add(self.a[:, :half], got_a), add(self.b[0], got_b)], axis=0)
        return got_a, got_b

    def hops(self, *first):
        bits = upper_bits(lax.axis_size("dp"))[::-1]
        for bit in bits:
            half = self.held.shape[-1] // 2
            got = exchange(self.held[:, half:], "dp", bit, *first)
            first = ()
            kept = self.held[:, :half]
            self.held = kept.astype(f32) + got.astype(f32) if bit == bits[-1] else add(kept, got)
        return self.held


def per_device(
    tokens,
    cotangent,
    segment_ids,
    positions,
    attention_entry,
    attention_exit,
    feedforward_entry,
    feedforward_exit,
    norm_gains,
    momentum_attention_entry,
    momentum_attention_exit,
    momentum_feedforward_entry,
    momentum_feedforward_exit,
    momentum_norm_gains,
    variance_attention_entry,
    variance_attention_exit,
    variance_feedforward_entry,
    variance_feedforward_exit,
    variance_norm_gains,
):
    own, width = tokens.shape
    local = attention_entry.shape[0]
    slice_width = attention_exit.shape[0]
    hidden = feedforward_exit.shape[0]
    pairs = slice_width // PAIR
    assert lax.axis_size("tensor") == 4 and own * 2 == LEN and segment_ids.shape[0] == 2 * LEN and pairs == 2
    lane = lax.axis_index("tensor")

    first_hidden = hidden // 2 // 16 * 16
    h1, h2 = first_hidden, hidden - first_hidden
    cut1, cut2 = h1 // 32 * 16, h2 // 32 * 16
    plan1 = ((("x", 0, slice_width), ("a", 0, h1)), (("b", 0, h1), ("f", 0, h1)))
    plan2 = ((("a", 0, h2), ("f", 0, cut2)), (("b", 0, h2), ("f", cut2, h2)))
    back1 = ((("a", 0, h1), ("b", 0, cut1)), (("b", cut1, h1), ("f", 0, h1)))
    back2 = plan2

    entry_rows = (
        attention_entry.astype(bf16)
        .reshape(local, 3, pairs, PAIR)
        .transpose(2, 1, 3, 0)
        .reshape(pairs * 3 * PAIR, local)
    )
    grow = feedforward_entry.transpose(1, 2, 0)
    owned = [
        {"a": grow[0, :h1], "b": grow[1, :h1], "f": feedforward_exit[:h1], "x": attention_exit},
        {"a": grow[0, h1:], "b": grow[1, h1:], "f": feedforward_exit[h1:]},
    ]

    def pack(rows, plan):
        return jnp.concatenate([rows[n][lo:hi] for side in plan for n, lo, hi in side], axis=0).astype(bf16)

    entry = Gather(entry_rows, 3 * PAIR)
    part1 = Gather(pack(owned[0], plan1), length(plan1[0]))
    part2 = Gather(pack(owned[1], plan2), length(plan2[0]))
    bits = upper_bits(lax.axis_size("dp"))
    gains_held = norm_gains.astype(bf16)
    arrived = ()
    for index, bit in enumerate(bits):
        got = entry.hop(bit)
        gains_held = lanes(gains_held, exchange(gains_held, "dp", bit))
        if index > 0:
            arrived = (part1.hop(bits[index - 1], got),)
    gains = lanes(gains_held, exchange(gains_held, "dp", 1)).astype(f32)
    got_cross = entry.cross()
    part1.hop(bits[-1], *got_cross)
    for index, bit in enumerate(bits):
        arrived = (part2.hop(bit, *arrived),)
    got_last = entry.finish()
    got1 = part1.cross(*got_last)
    part1.finish()
    got1 = (part1.other_a, part1.b)
    part2.cross(*got1)
    part2.finish()

    block, places = column_blocks(width)
    x, cot_own, n1_own = enter(block, places, flip_columns(tokens, False), flip_columns(cotangent, False), gains)
    n1 = (n1_own, swap_core(n1_own))
    cot = (cot_own, swap_core(cot_own))

    def rows_of(vector):
        first = lax.dynamic_slice_in_dim(vector, lane * own, own, 0)
        second = lax.dynamic_slice_in_dim(vector, (lane ^ 1) * own, own, 0)
        return jnp.concatenate([first, second])

    segments = rows_of(segment_ids)
    tables = rope_tables(rows_of(positions)) + (segments[None, :], segments[:, None])

    w_entry = (entry.a[None], entry.other_a[None], entry.b)
    kept = [attend(*n1, w, tables) for w in w_entry]
    w1, w2 = part1.arrays(), part2.arrays()
    part_own, part_send = branch([k[1] for k in kept], w1[0], pairs)
    h, n2_own = middle(x, part_own, swap_core(part_send), gains)
    n2 = (n2_own, swap_core(n2_own))
    out_sum, dn_sum, *grads1 = feed(n2, cot, w1, (), plan1, back1)
    out_own, out_send, dn_own, dn_send, *grads2 = feed(n2, cot, w2, (out_sum, dn_sum), plan2, back2)

    sum1 = Scatter(grads1[0][0], grads1[0][1], *grads1[1:])
    sum2 = Scatter(grads2[0][0], grads2[0][1], *grads2[1:])
    got1 = sum1.start()
    got1 = sum1.cross()
    dn_got = swap_core(dn_send)
    got2 = sum2.start(*got1)
    g_feed1 = sum1.hops()
    got2 = sum2.cross()
    g_feed2 = sum2.hops()
    dh, dh_own, gain_two = turn(h, dn_own, dn_got, cot_own, gains)
    grads = (dh_own, swap_core(dh_own))
    spots = (lambda i: (0, 0), lambda i: (1, 0), lambda i: (i, 1))

    def back(g):
        return attend_back(n1, grads, w1[0], spots[g], *kept[g], tables)

    dp_other, low_other, high_other = back(1)
    dp_both, low_both, high_both = back(2)
    dp_own, low_own, high_own = back(0)
    sum0 = Scatter(lanes(low_own[0], high_own[0]), lanes(low_other[0], high_other[0]), low_both, high_both)
    sum0.start()
    sum0.cross()
    g_entry = sum0.hops()
    n_own, n_send = last((dp_own, dp_other, dp_both), w_entry)
    n_got = swap_core(n_send)
    input_gradient, gain_one = leave(block, places, x, n_own, n_got, dh, gains)
    input_gradient = flip_columns(input_gradient, True)
    block_output = flip_columns(result(block, places, h, out_own, swap_core(out_send)), True)

    gains_local = jnp.concatenate([gain_one, gain_two], axis=0)
    for bit in [1] + bits[::-1]:
        half = gains_local.shape[1] // 2
        gains_local = gains_local[:, :half] + exchange(gains_local[:, half:], "dp", bit)
    gains_gradient = tree_sum(gains_local, "tensor")
    by_pair = g_entry.reshape(pairs, 4 * PAIR, local)
    entry_gradient = (
        by_pair[:, : 3 * PAIR].reshape(pairs, 3, PAIR, local).transpose(3, 1, 0, 2).reshape(local, 3, slice_width)
    )
    exit_gradient = by_pair[:, 3 * PAIR :].reshape(slice_width, local)

    def unpack(value, plan, name):
        at, found = 0, []
        for side in plan:
            for label, lo, hi in side:
                if label == name:
                    found.append((lo, value[at : at + hi - lo]))
                at += hi - lo
        return [rows for _, rows in sorted(found, key=lambda f: f[0])]

    def both(name):
        return jnp.concatenate(unpack(g_feed1, back1, name) + unpack(g_feed2, back2, name), axis=0)

    grow_gradient = jnp.stack([both("a"), both("b")]).transpose(2, 0, 1)
    gradients = (entry_gradient, exit_gradient, grow_gradient, both("f"), gains_gradient)

    masters = (attention_entry, attention_exit, feedforward_entry, feedforward_exit, norm_gains)
    momenta = (
        momentum_attention_entry,
        momentum_attention_exit,
        momentum_feedforward_entry,
        momentum_feedforward_exit,
        momentum_norm_gains,
    )
    variances = (
        variance_attention_entry,
        variance_attention_exit,
        variance_feedforward_entry,
        variance_feedforward_exit,
        variance_norm_gains,
    )
    first_tensor = (lane == 0).astype(f32)
    shares = (1.0, 1.0, 1.0, 1.0, first_tensor)
    states = []
    square_rows = []
    for master, gradient, momentum, variance, share in zip(masters, gradients, momenta, variances, shares):
        new_momentum, new_variance, update = lamb_direction(master, gradient, momentum, variance)
        states.append((new_momentum, new_variance, update))
        square_rows.append(jnp.stack([jnp.sum(master * master), jnp.sum(update * update)]) * share)
    totals = tree_sum(tree_sum(jnp.stack(square_rows), "tensor"), "dp")
    updated_all = []
    for index in range(5):
        ratio = jnp.sqrt(totals[index, 0] / (totals[index, 1] + ratio_eps))
        updated_all.append(masters[index] - learn_rate * ratio * states[index][2])
    outputs = [block_output, input_gradient]
    for index in range(5):
        outputs += [gradients[index], updated_all[index], states[index][0], states[index][1]]
    return tuple(outputs + [jnp.sqrt(totals)])


def solution(mesh):
    rows = P(("dp", "tensor"), None)
    first = P("dp", None, "tensor")
    second = P("tensor", "dp")
    gains = P(None, "dp")
    weights = (first, second, first, second, gains)
    in_specs = (rows, rows, P("dp"), P("dp")) + weights * 3
    out_specs = (rows, rows) + tuple(spec for spec in weights for _ in range(4)) + (P(),)
    return jax.shard_map(per_device, mesh=mesh, in_specs=in_specs, out_specs=out_specs, check_vma=False)
```
